32 devices in a mesh: dp: 8 (over z, x), tensor: 4 (over y, core).
Axes of the slice: x: 2, y: 2, z: 4, core: 2. Of those that a mesh axis runs over, the one named last changes fastest.
Arguments:
- tokens: bfloat16 [16, 512, 1024], P('dp'), may hold values from -6 to 6
- cotangent: bfloat16 [16, 512, 1024], P('dp'), may hold values from -6 to 6
- lengths: int32 [16], P('dp'), may hold values from 64 to 512, as said below
- qkv_weight: bfloat16 [1024, 3, 1024], P('dp', None, 'tensor'), may hold values from -0.1875 to 0.1875
- qv_bias: bfloat16 [16, 128], P('tensor', 'dp'), may hold values from -3 to 3
- out_weight: bfloat16 [1024, 1024], P('tensor', 'dp'), may hold values from -2 to 2
- out_bias: bfloat16 [1024], P('dp'), may hold values from -3 to 3
- first_gain: bfloat16 [1024], P('dp'), may hold values from 0.5 to 1.5
- first_shift: bfloat16 [1024], P('dp'), may hold values from -3 to 3
- up_weight: bfloat16 [1024, 4096], P('dp', 'tensor'), may hold values from -0.1875 to 0.1875
- up_bias: bfloat16 [32, 128], P('tensor', 'dp'), may hold values from -3 to 3
- down_weight: bfloat16 [4096, 1024], P('tensor', 'dp'), may hold values from -0.09375 to 0.09375
- down_bias: bfloat16 [1024], P('dp'), may hold values from -3 to 3
- second_gain: bfloat16 [1024], P('dp'), may hold values from 0.5 to 1.5
- second_shift: bfloat16 [1024], P('dp'), may hold values from -3 to 3
Outputs:
- result: bfloat16 [16, 512, 1024], P('dp', 'tensor')
- grad_tokens: float32 [16, 512, 1024], P('dp', 'tensor')
- grad_qkv: float32 [1024, 3, 1024], P('dp', None, 'tensor')
- grad_qv_bias: float32 [16, 128], P('tensor', 'dp')
- grad_out_weight: float32 [1024, 1024], P('tensor', 'dp')
- grad_out_bias: float32 [1024], P('dp')
- grad_first_gain: float32 [1024], P('dp')
- grad_first_shift: float32 [1024], P('dp')
- grad_up_weight: float32 [1024, 4096], P('dp', 'tensor')
- grad_up_bias: float32 [32, 128], P('tensor', 'dp')
- grad_down_weight: float32 [4096, 1024], P('tensor', 'dp')
- grad_down_bias: float32 [1024], P('dp')
- grad_second_gain: float32 [1024], P('dp')
- grad_second_shift: float32 [1024], P('dp')
The draws below stay inside these ranges and needn't reach their ends.
Inputs may be any that keep to these rules, and one draw needn't show every extreme that they name: `lengths`: real length of each sequence; the first sequence has the full length 512 and the last one the least length, 64. Positions at or past the length are padding.
All inputs are finite; a program needn't handle non-finite values.
Results may differ from the reference program's by a relative error of at most 0.02.
Values may be sent and summed in bfloat16 or wider, within the bound.
No kernel may reach another device: no remote copies, remote signals or barrier semaphores. Data moves between devices by JAX's collectives and lax.ppermute only.
A program may use at most 128 MiB of HBM per device.

```python
import jax
import jax.numpy as jnp
from jax import lax

D = 1024
HEADS = 16
HD = 64
FF = 4096
SEQ_LEN = 512
BCOL = 128
SEQ_DEV = 2
SEQS = 16


def draw_lengths(key, part):
    level_key = jax.random.fold_in(key, 11)
    trim_key = jax.random.fold_in(key, 12)
    levels = jax.random.randint(level_key, (SEQS // SEQ_DEV,), 8, 61)
    trims = jax.random.randint(trim_key, (SEQS,), 0, SEQ_LEN)
    spread = jnp.repeat(levels, SEQ_DEV)
    least = max(1, SEQ_LEN // 8)
    lengths = jnp.maximum(SEQ_LEN - trims * spread // 64, least)
    lengths = lengths.at[SEQS - 1].set(least)
    return lengths.at[0].set(SEQ_LEN).astype(jnp.int32)


def block_scale(rng, shape, split, low, high):
    def one(dim, shards_of):
        draws = jax.random.uniform(jax.random.fold_in(jax.random.fold_in(rng, 6), dim), (shards_of,), jnp.float32, low / len(split), high / len(split))
        return jnp.repeat(jnp.exp(draws), shape[dim] // shards_of).reshape((-1,) + (1,) * (len(shape) - dim - 1))

    level = one(*split[0])
    for cut in split[1:]:
        level = level * one(*cut)
    return level


def centred(own_key, extent, scale, most, split=(), kind=jnp.bfloat16):
    level = block_scale(own_key, extent, split, -0.22, 0.18) if split else 1.0
    result = jax.random.normal(own_key, extent, jnp.float32) * scale * level
    return jnp.minimum(jnp.maximum(result, -most), most).astype(kind)


def setup_inputs(seed: int = 0) -> dict:
    seeds = jax.random.split(jax.random.key(seed), 16)
    tokens = centred(seeds[0], (SEQS, SEQ_LEN, D), 1.0, 6.0, ((0, 8),))
    cotangent = centred(seeds[1], (SEQS, SEQ_LEN, D), 1.0, 6.0, ((0, 8),))
    lengths = draw_lengths(jax.random.fold_in(seeds[15], 71), 0)
    qkv_weight = centred(seeds[3], (D, 3, D), D ** -0.5, 0.1875, ((0, 8), (2, 4)))
    qv_bias = centred(seeds[4], (HEADS, 2 * HD), 0.5, 3.0, ((0, 4), (1, 8)))
    out_weight = centred(seeds[5], (D, D), (max(1, D * 4 // SEQ_LEN)) ** -0.5, 2.0, ((0, 4), (1, 8)))
    out_bias = centred(seeds[6], (D,), 0.5, 3.0, ((0, 8),))
    first_gain = jnp.clip(1.0 + 0.1 * jax.random.normal(seeds[7], (D,), jnp.float32), 0.5, 1.5).astype(jnp.bfloat16)
    first_shift = centred(seeds[8], (D,), 0.5, 3.0, ((0, 8),))
    up_weight = centred(seeds[9], (D, FF), D ** -0.5, 0.1875, ((0, 8), (1, 4)))
    up_bias = centred(seeds[10], (FF // BCOL, BCOL), 0.5, 3.0, ((0, 4), (1, 8)))
    down_weight = centred(seeds[11], (FF, D), FF ** -0.5, 0.09375, ((0, 4), (1, 8)))
    down_bias = centred(seeds[12], (D,), 0.5, 3.0, ((0, 8),))
    second_gain = jnp.clip(1.0 + 0.1 * jax.random.normal(seeds[13], (D,), jnp.float32), 0.5, 1.5).astype(jnp.bfloat16)
    second_shift = centred(seeds[14], (D,), 0.5, 3.0, ((0, 8),))
    return {"tokens": tokens, "cotangent": cotangent, "lengths": lengths, "qkv_weight": qkv_weight, "qv_bias": qv_bias, "out_weight": out_weight, "out_bias": out_bias, "first_gain": first_gain, "first_shift": first_shift, "up_weight": up_weight, "up_bias": up_bias, "down_weight": down_weight, "down_bias": down_bias, "second_gain": second_gain, "second_shift": second_shift}


EPSILON = 1e-12
NEG_LARGE = -1e+30

def norm_forward(summed, gain, shift):
    centre = summed - lax.optimization_barrier(jnp.mean(summed, axis=-1, keepdims=True))
    inverse = lax.rsqrt(lax.optimization_barrier(jnp.mean(centre * centre, axis=-1, keepdims=True)) + EPSILON)
    normed = centre * inverse
    return (normed * gain + shift, normed, inverse)

def norm_backward(upstream, normed, inverse, gain):
    scaled = upstream * gain
    back = inverse * (scaled - lax.optimization_barrier(jnp.mean(scaled, axis=-1, keepdims=True)) - normed * lax.optimization_barrier(jnp.mean(scaled * normed, axis=-1, keepdims=True)))
    return (back, lax.optimization_barrier(jnp.sum(upstream * normed, axis=0)), lax.optimization_barrier(jnp.sum(upstream, axis=0)))

def gelu_slope(pre_act):
    lower = 0.5 * (1.0 + jax.scipy.special.erf(pre_act * 0.7071067811865476))
    density = jnp.exp(-0.5 * pre_act * pre_act) * 0.3989422804014327
    return lower + pre_act * density

def one_sequence(params, tokens_one, cotangent_one, length_one):
    qkv_flat, query_bias, value_bias, out_weight, out_bias, first_gain, first_shift, up_weight, up_bias, down_weight, down_bias, second_gain, second_shift = params
    scale = HD ** (-0.5)
    positions = jnp.arange(SEQ_LEN, dtype=jnp.int32)
    valid = positions < length_one
    row_valid = valid[:, None]
    projected = jnp.dot(tokens_one, qkv_flat, preferred_element_type=jnp.float32).reshape(SEQ_LEN, 3, D)
    head_shape = (SEQ_LEN, HEADS, HD)
    queries = (projected[:, 0] + query_bias).astype(jnp.bfloat16).reshape(head_shape)
    keys_low = projected[:, 1].astype(jnp.bfloat16).reshape(head_shape)
    values_low = (projected[:, 2] + value_bias).astype(jnp.bfloat16).reshape(head_shape)
    query_wide = queries.astype(jnp.float32)
    key_wide = keys_low.astype(jnp.float32)
    value_wide = values_low.astype(jnp.float32)
    scores = jnp.einsum('qhe,khe->hqk', query_wide, key_wide) * scale
    scores = jnp.where(valid[None, None, :], scores, NEG_LARGE)
    log_total = jnp.log(lax.optimization_barrier(jnp.sum(jnp.exp(scores), axis=-1, keepdims=True)))
    weights = jnp.exp(scores - log_total)
    weights_low = weights.astype(jnp.bfloat16)
    weights_wide = weights_low.astype(jnp.float32)
    context = jnp.einsum('hqk,khe->qhe', weights_wide, value_wide).reshape(SEQ_LEN, D).astype(jnp.bfloat16)
    first_sum = tokens_one.astype(jnp.float32) + jnp.dot(context, out_weight, preferred_element_type=jnp.float32) + out_bias
    hidden, normed_one, inverse_one = norm_forward(first_sum, first_gain, first_shift)
    hidden_low = hidden.astype(jnp.bfloat16)
    pre_act = jnp.dot(hidden_low, up_weight, preferred_element_type=jnp.float32) + up_bias
    act_low = jax.nn.gelu(pre_act, approximate=False).astype(jnp.bfloat16)
    second_sum = hidden + jnp.dot(act_low, down_weight, preferred_element_type=jnp.float32) + down_bias
    normed_out, normed_two, inverse_two = norm_forward(second_sum, second_gain, second_shift)
    result_one = jnp.where(row_valid, normed_out, 0.0).astype(jnp.bfloat16)
    upstream = jnp.where(row_valid, cotangent_one.astype(jnp.float32), 0.0)
    back_two, grad_second_gain, grad_second_shift = norm_backward(upstream, normed_two, inverse_two, second_gain)
    grad_down_bias = lax.optimization_barrier(jnp.sum(back_two, axis=0))
    back_two_low = back_two.astype(jnp.bfloat16)
    grad_down = jnp.dot(act_low.T, back_two_low, preferred_element_type=jnp.float32)
    back_act = jnp.dot(back_two_low, down_weight.T, preferred_element_type=jnp.float32)
    back_pre = back_act * gelu_slope(pre_act)
    grad_up_bias = lax.optimization_barrier(jnp.sum(back_pre, axis=0))
    back_pre_low = back_pre.astype(jnp.bfloat16)
    grad_up = jnp.dot(hidden_low.T, back_pre_low, preferred_element_type=jnp.float32)
    back_hidden = back_two + jnp.dot(back_pre_low, up_weight.T, preferred_element_type=jnp.float32)
    back_one, grad_first_gain, grad_first_shift = norm_backward(back_hidden, normed_one, inverse_one, first_gain)
    grad_out_bias = lax.optimization_barrier(jnp.sum(back_one, axis=0))
    back_one_low = back_one.astype(jnp.bfloat16)
    grad_out = jnp.dot(context.T, back_one_low, preferred_element_type=jnp.float32)
    back_context = jnp.dot(back_one_low, out_weight.T, preferred_element_type=jnp.float32).astype(jnp.bfloat16)
    back_wide = back_context.reshape(head_shape).astype(jnp.float32)
    grad_values = jnp.einsum('hqk,qhe->khe', weights_wide, back_wide)
    back_weights = jnp.einsum('qhe,khe->hqk', back_wide, value_wide)
    back_scores = weights * (back_weights - lax.optimization_barrier(jnp.sum(weights * back_weights, axis=-1, keepdims=True))) * scale
    back_scores_wide = back_scores.astype(jnp.bfloat16).astype(jnp.float32)
    grad_queries = jnp.einsum('hqk,khe->qhe', back_scores_wide, key_wide)
    grad_keys = jnp.einsum('hqk,qhe->khe', back_scores_wide, query_wide)
    grad_query_bias = lax.optimization_barrier(jnp.sum(grad_queries, axis=0)).reshape(D)
    grad_value_bias = lax.optimization_barrier(jnp.sum(grad_values, axis=0)).reshape(D)
    back_qkv = jnp.stack([grad_queries.reshape(SEQ_LEN, D), grad_keys.reshape(SEQ_LEN, D), grad_values.reshape(SEQ_LEN, D)], axis=1)
    back_qkv = back_qkv.reshape(SEQ_LEN, 3 * D).astype(jnp.bfloat16)
    grad_qkv = jnp.dot(tokens_one.T, back_qkv, preferred_element_type=jnp.float32)
    grad_tokens_one = back_one + jnp.dot(back_qkv, qkv_flat.T, preferred_element_type=jnp.float32)
    grads = (grad_qkv, grad_query_bias, grad_value_bias, grad_out, grad_out_bias, grad_first_gain, grad_first_shift, grad_up, grad_up_bias, grad_down, grad_down_bias, grad_second_gain, grad_second_shift)
    return (result_one, grad_tokens_one, grads)

def reference(tokens, cotangent, lengths, qkv_weight, qv_bias, out_weight, out_bias, first_gain, first_shift, up_weight, up_bias, down_weight, down_bias, second_gain, second_shift):
    params = (qkv_weight.reshape(D, 3 * D), qv_bias[:, :HD].reshape(D).astype(jnp.float32), qv_bias[:, HD:].reshape(D).astype(jnp.float32), out_weight, out_bias.astype(jnp.float32), first_gain.astype(jnp.float32), first_shift.astype(jnp.float32), up_weight, up_bias.reshape(FF).astype(jnp.float32), down_weight, down_bias.astype(jnp.float32), second_gain.astype(jnp.float32), second_shift.astype(jnp.float32))
    initial = (jnp.zeros((D, 3 * D), jnp.float32), jnp.zeros((D,), jnp.float32), jnp.zeros((D,), jnp.float32), jnp.zeros((D, D), jnp.float32), jnp.zeros((D,), jnp.float32), jnp.zeros((D,), jnp.float32), jnp.zeros((D,), jnp.float32), jnp.zeros((D, FF), jnp.float32), jnp.zeros((FF,), jnp.float32), jnp.zeros((FF, D), jnp.float32), jnp.zeros((D,), jnp.float32), jnp.zeros((D,), jnp.float32), jnp.zeros((D,), jnp.float32))

    def advance(carry, items):
        result_one, grad_tokens_one, grads = one_sequence(params, items[0], items[1], items[2])
        return (jax.tree.map(jnp.add, carry, grads), (result_one, grad_tokens_one))
    totals, outputs = lax.scan(advance, initial, (tokens, cotangent, lengths))
    grad_qv_bias = jnp.concatenate([totals[1].reshape(HEADS, HD), totals[2].reshape(HEADS, HD)], axis=1)
    return (outputs[0], outputs[1], totals[0].reshape(D, 3, D), grad_qv_bias, totals[3], totals[4], totals[5], totals[6], totals[7], totals[8].reshape(FF // BCOL, BCOL), totals[9], totals[10], totals[11], totals[12])
```

```python
from functools import partial

import jax
import jax.numpy as jnp
from jax import lax
from jax.experimental import pallas as pl
from jax.experimental.pallas import tpu as pltpu
from jax.sharding import PartitionSpec as P

EPSILON = 1e-12
NEG_LARGE = -1e30
F32 = jnp.float32
BF16 = jnp.bfloat16

ORDER = (0, 2, 1, 3)
CORE = [(i, i ^ 1) for i in range(4)]
SIDE = [(i, i ^ 2) for i in range(4)]


def norm_forward(summed, gain, shift):
    centre = summed - jnp.mean(summed, axis=-1, keepdims=True)
    inverse = lax.rsqrt(jnp.mean(centre * centre, axis=-1, keepdims=True) + EPSILON)
    normed = centre * inverse
    return (normed * gain + shift, normed, inverse)


def norm_backward(upstream, normed, inverse, gain):
    scaled = upstream * gain
    return inverse * (
        scaled
        - jnp.mean(scaled, axis=-1, keepdims=True)
        - normed * jnp.mean(scaled * normed, axis=-1, keepdims=True)
    )


def gelu_slope(pre_act):
    lower = 0.5 * (1.0 + jax.scipy.special.erf(pre_act * 0.7071067811865476))
    density = jnp.exp(-0.5 * pre_act * pre_act) * 0.3989422804014327
    return lower + pre_act * density


def matmul(a, b, dims=((1,), (0,))):
    return lax.dot_general(a, b, (dims, ((), ())), preferred_element_type=F32)


NT = ((1,), (1,))
TN = ((0,), (0,))


def positions(group, shape, axis, share):
    index = lax.broadcasted_iota(jnp.int32, shape, axis)
    block = index // share
    step = jnp.where(block == 1, 2, jnp.where(block == 2, 1, block))
    return (group ^ step) * share + index % share


def attention_kernel(info, proj, out, *, heads, share):
    length, wide = proj.shape
    width = wide // 3
    size = width // heads
    half = width // 2
    lane = lax.broadcasted_iota(jnp.int32, (1, width), 1)
    half_lane = lax.broadcasted_iota(jnp.int32, (1, half), 1)
    bias = jnp.where(positions(info[0], (1, length), 1, share) < info[1], 0.0, NEG_LARGE)
    scale = size ** (-0.5)
    queries = proj[:, :width]
    keys = proj[:, width : 2 * width]
    values = proj[:, 2 * width :]
    halves = []
    for side in range(2):
        own = slice(side * half, (side + 1) * half)
        other = slice((1 - side) * half, (2 - side) * half)
        joined = jnp.zeros((length, half), F32)
        for inner in range(heads // 2):
            head = side * (heads // 2) + inner
            mine = (lane // size) == head
            scores = matmul(jnp.where(mine, queries, BF16(0)), keys, NT) * scale + bias
            terms = jnp.exp(scores).astype(BF16)
            summed = matmul(terms, jnp.where(mine, values, BF16(1)))
            joined = jnp.where(
                (half_lane // size) == inner, summed[:, own] / summed[:, other], joined
            )
        halves.append(joined)
    out[...] = jnp.concatenate(halves, axis=1).astype(BF16)


def attention_back_kernel(info, proj, back, out, *, heads, share):
    length, wide = proj.shape
    width = wide // 3
    size = width // heads
    scale = size ** (-0.5)
    lane = lax.broadcasted_iota(jnp.int32, (1, width), 1)
    bias = jnp.where(positions(info[0], (length, 1), 0, share) < info[1], 0.0, NEG_LARGE)
    queries = proj[:, :width]
    keys = proj[:, width : 2 * width]
    values = proj[:, 2 * width :]
    upstream = back[...]
    zero = BF16(0)
    grad_q = jnp.zeros((length, width), F32)
    grad_k = jnp.zeros((length, width), F32)
    grad_v = jnp.zeros((length, width), F32)
    for head in range(heads):
        mine = (lane // size) == head
        head_q = jnp.where(mine, queries, zero)
        head_k = jnp.where(mine, keys, zero)
        head_up = jnp.where(mine, upstream, zero)
        terms = jnp.exp(matmul(keys, head_q, NT) * scale + bias)
        weights = terms * (1.0 / jnp.sum(terms, axis=0, keepdims=True))
        back_weights = matmul(values, head_up, NT)
        product = weights * back_weights
        scores = product - weights * jnp.sum(product, axis=0, keepdims=True)
        scores = (scores * scale).astype(BF16)
        grad_v = grad_v + matmul(weights.astype(BF16), head_up)
        grad_k = grad_k + matmul(scores, head_q)
        grad_q = grad_q + matmul(scores, head_k, TN)
    out[:, :width] = grad_q
    out[:, width : 2 * width] = grad_k
    out[:, 2 * width :] = grad_v


def attention(info, proj, heads, share):
    length, wide = proj.shape
    width = wide // 3
    return pl.pallas_call(
        partial(attention_kernel, heads=heads, share=share),
        out_shape=jax.ShapeDtypeStruct((length, width), BF16),
        in_specs=[
            pl.BlockSpec(memory_space=pltpu.SMEM),
            pl.BlockSpec(memory_space=pltpu.VMEM),
        ],
        out_specs=pl.BlockSpec(memory_space=pltpu.VMEM),
        cost_estimate=pl.CostEstimate(
            flops=4 * length * length * width * heads,
            bytes_accessed=8 * length * width,
            transcendentals=heads * length * length,
        ),
        name="attention",
    )(info, proj)


def attention_back(info, proj, back, heads, share):
    length, wide = proj.shape
    width = wide // 3
    return pl.pallas_call(
        partial(attention_back_kernel, heads=heads, share=share),
        out_shape=jax.ShapeDtypeStruct((length, wide), F32),
        in_specs=[
            pl.BlockSpec(memory_space=pltpu.SMEM),
            pl.BlockSpec(memory_space=pltpu.VMEM),
            pl.BlockSpec(memory_space=pltpu.VMEM),
        ],
        out_specs=pl.BlockSpec(memory_space=pltpu.VMEM),
        cost_estimate=pl.CostEstimate(
            flops=10 * length * length * width * heads,
            bytes_accessed=20 * length * width,
            transcendentals=heads * length * length,
        ),
        name="attention_back",
    )(info, proj, back)


def gather_rows(own):
    side = lax.ppermute(own, "tensor", SIDE)
    near = jnp.concatenate([own, side], axis=0)
    far = lax.ppermute(near, "tensor", CORE)
    return jnp.concatenate([near, far], axis=0)


def scatter_rows(terms):
    half = terms.shape[0] // 2
    share = half // 2
    there = lax.ppermute(terms[half:].astype(BF16), "tensor", CORE)
    near = terms[:half] + there.astype(F32)
    side = lax.ppermute(near[share:].astype(BF16), "tensor", SIDE)
    return near[:share] + side.astype(F32)


def tensor_sum(value):
    value = value + lax.ppermute(value, "tensor", CORE)
    return value + lax.ppermute(value, "tensor", SIDE)


def owners(index, count):
    planes = count // 2
    plane, side = index // 2, index % 2
    return [
        [((plane + step) % planes) * 2 + (side ^ flip) for flip in range(2)]
        for step in range(planes)
    ]


def gather_shards(shard, count):
    planes = count // 2
    pair = [(i, i ^ 1) for i in range(count)]
    pieces = [shard]
    for step in range(1, planes):
        ring = [(i, (i + 2 * step) % count) for i in range(count)]
        pieces.append(lax.ppermute(shard, "dp", ring))
    return [[piece, lax.ppermute(piece, "dp", pair)] for piece in pieces]


def scatter_shards(pieces, count):
    planes = count // 2
    pair = [(i, i ^ 1) for i in range(count)]
    away = jnp.stack([pieces[step][1] for step in range(planes)]).astype(BF16)
    away = lax.ppermute(away, "dp", pair)
    near = [pieces[step][0] + away[step].astype(F32) for step in range(planes)]
    total = near[0]
    for step in range(1, planes):
        ring = [(i, (i + 2 * step) % count) for i in range(count)]
        total = total + lax.ppermute(near[step].astype(BF16), "dp", ring).astype(F32)
    return total


def body(
    tokens,
    cotangent,
    lengths,
    qkv_weight,
    qv_bias,
    out_weight,
    out_bias,
    first_gain,
    first_shift,
    up_weight,
    up_bias,
    down_weight,
    down_bias,
    second_gain,
    second_shift,
):
    seqs, length, width = tokens.shape
    groups = lax.axis_size("tensor")
    count = lax.axis_size("dp")
    share = length // groups
    group = lax.axis_index("tensor")
    index = lax.axis_index("dp")
    part = width // count
    local = qkv_weight.shape[2]
    units = up_weight.shape[1]
    heads = qv_bias.shape[0]
    size = local // heads
    rows_bias = up_bias.shape[0]
    cols_bias = up_bias.shape[1]
    cols_qv = qv_bias.shape[1]

    wide_params = [out_bias, first_gain, first_shift, down_bias, second_gain, second_shift]
    small = jnp.concatenate([p.reshape(-1) for p in wide_params + [up_bias, qv_bias]])
    small_rows = -(-small.shape[0] // (16 * part)) * 16
    small = jnp.pad(small, (0, small_rows * part - small.shape[0])).reshape(small_rows, part)
    blocks = 3 * local // part
    first_pack = jnp.concatenate(
        [
            qkv_weight.reshape(part, blocks, part).transpose(1, 0, 2).reshape(blocks * part, part),
            out_weight,
            small,
        ]
    )
    lines = units * part // width
    second_pack = jnp.concatenate(
        [
            up_weight,
            down_weight.reshape(units // lines, lines, part).transpose(1, 0, 2).reshape(lines, -1)
        ]
    )
    gathered = lax.all_gather(second_pack, "dp", axis=0, tiled=False)

    pieces = gather_shards(first_pack, count)
    planes = count // 2
    packed = jnp.zeros((count,) + first_pack.shape, BF16)
    for step in range(planes):
        for flip in range(2):
            source = ((index // 2 - step) % planes) * 2 + ((index % 2) ^ flip)
            packed = lax.dynamic_update_slice(packed, pieces[step][flip][None], (source, 0, 0))
    qkv_full = (
        packed[:, : blocks * part]
        .reshape(count, blocks, part, part)
        .transpose(0, 2, 1, 3)
        .reshape(width, 3 * local)
    )
    out_full = (
        packed[:, blocks * part : blocks * part + local].transpose(1, 0, 2).reshape(local, width)
    )
    small = packed[:, blocks * part + local :].reshape(count, -1)
    wide = small[:, : 6 * part].astype(F32).reshape(count, 6, part).transpose(1, 0, 2)
    wide = wide.reshape(6, 1, width)
    out_bias_full, gain_one, shift_one, down_bias_full, gain_two, shift_two = wide
    at = 6 * part
    up_bias_row = small[:, at : at + rows_bias * cols_bias].reshape(count, rows_bias, cols_bias)
    up_bias_row = up_bias_row.transpose(1, 0, 2).reshape(1, units).astype(F32)
    at = at + rows_bias * cols_bias
    qv_full = small[:, at : at + heads * cols_qv].reshape(count, heads, cols_qv)
    qv_full = qv_full.transpose(1, 0, 2).reshape(heads, 2 * size).astype(F32)
    proj_bias = jnp.concatenate(
        [
            qv_full[:, :size].reshape(1, local),
            jnp.zeros((1, local), F32),
            qv_full[:, size:].reshape(1, local),
        ],
        axis=1,
    )

    up_full = gathered[:, :part].reshape(width, units)
    down_full = (
        gathered[:, part:]
        .reshape(count, lines, units // lines, part)
        .transpose(2, 1, 0, 3)
        .reshape(units, width)
    )

    quarters = tokens.reshape(seqs, groups, share, width)
    own_tokens = lax.dynamic_index_in_dim(quarters, group, 1, keepdims=False)
    ordered = jnp.concatenate(
        [lax.dynamic_slice_in_dim(quarters, group ^ step, 1, 1) for step in ORDER], axis=1
    ).reshape(seqs, length, width)
    own_cotangent = lax.dynamic_index_in_dim(
        cotangent.reshape(seqs, groups, share, width), group, 1, keepdims=False
    )
    own_at = group * share + lax.broadcasted_iota(jnp.int32, (share, 1), 0)

    every = range(seqs)
    info = [jnp.stack([group, lengths[s]]).astype(jnp.int32) for s in every]
    own_valid = [own_at < lengths[s] for s in every]
    proj = [(matmul(ordered[s], qkv_full) + proj_bias).astype(BF16) for s in every]
    context = [attention(info[s], proj[s], heads, share) for s in every]
    attended = [scatter_rows(matmul(context[s], out_full)) for s in every]
    one = [
        norm_forward(
            own_tokens[s].astype(F32) + attended[s] + out_bias_full, gain_one, shift_one
        )
        for s in every
    ]
    hidden_low = [gather_rows(one[s][0].astype(BF16)) for s in every]
    pre_act = [matmul(hidden_low[s], up_full) + up_bias_row for s in every]
    act_low = [jax.nn.gelu(pre_act[s], approximate=False).astype(BF16) for s in every]
    fed = [scatter_rows(matmul(act_low[s], down_full)) for s in every]
    two = [
        norm_forward(one[s][0] + fed[s] + down_bias_full, gain_two, shift_two) for s in every
    ]
    result = jnp.stack(
        [jnp.where(own_valid[s], two[s][0], 0.0).astype(BF16) for s in every]
    )
    upstream = [jnp.where(own_valid[s], own_cotangent[s].astype(F32), 0.0) for s in every]
    back_two = [norm_backward(upstream[s], two[s][1], two[s][2], gain_two) for s in every]
    back_two_low = [gather_rows(back_two[s].astype(BF16)) for s in every]
    back_pre = [
        matmul(back_two_low[s], down_full, NT) * gelu_slope(pre_act[s]) for s in every
    ]
    grad_up_bias = sum(jnp.sum(back_pre[s], axis=0) for s in every)
    back_pre_low = [back_pre[s].astype(BF16) for s in every]
    up_terms = [scatter_rows(matmul(back_pre_low[s], up_full, NT)) for s in every]
    back_hidden = [back_two[s] + up_terms[s] for s in every]
    back_one = [norm_backward(back_hidden[s], one[s][1], one[s][2], gain_one) for s in every]
    back_one_low = [gather_rows(back_one[s].astype(BF16)) for s in every]
    back_context = [matmul(back_one_low[s], out_full, NT).astype(BF16) for s in every]

    both = lambda parts: jnp.concatenate(parts, axis=0)
    back_two_all = both(back_two_low)
    grad_down = matmul(both(act_low), back_two_all, TN).astype(BF16)
    grad_up = matmul(both(hidden_low), both(back_pre_low), TN).astype(BF16)
    grad_out = matmul(both(context), both(back_one_low), TN).astype(BF16)
    out_lines = local * part // width
    bulk = jnp.concatenate(
        [
            grad_up.reshape(count, part, units),
            grad_down.reshape(units // lines, lines, count, part)
            .transpose(2, 1, 0, 3)
            .reshape(count, lines, width),
            grad_out.reshape(local // out_lines, out_lines, count, part)
            .transpose(2, 1, 0, 3)
            .reshape(count, out_lines, width),
        ],
        axis=1,
    )
    bulk = lax.psum_scatter(bulk, "dp", scatter_dimension=0, tiled=False).astype(F32)

    back_qkv = [
        attention_back(info[s], proj[s], back_context[s], heads, share) for s in every
    ]
    qkv_sums = sum(jnp.sum(back_qkv[s], axis=0) for s in every)
    grad_qv = jnp.concatenate(
        [qkv_sums[:local].reshape(heads, size), qkv_sums[2 * local :].reshape(heads, size)],
        axis=1,
    )
    back_qkv_low = [back_qkv[s].astype(BF16) for s in every]
    input_sum = [scatter_rows(matmul(back_qkv_low[s], qkv_full, NT)) for s in every]
    grad_tokens = jnp.stack([back_one[s] + input_sum[s] for s in every])

    small_terms = jnp.stack(
        [
            sum(jnp.sum(back_one[s], axis=0) for s in every),
            sum(jnp.sum(back_hidden[s] * one[s][1], axis=0) for s in every),
            sum(jnp.sum(back_hidden[s], axis=0) for s in every),
            sum(jnp.sum(back_two[s], axis=0) for s in every),
            sum(jnp.sum(upstream[s] * two[s][1], axis=0) for s in every),
            sum(jnp.sum(upstream[s], axis=0) for s in every),
        ]
    )
    small_terms = tensor_sum(small_terms)
    small_grads = jnp.concatenate(
        [
            small_terms.reshape(6, count, part).transpose(1, 0, 2).reshape(count, 6 * part),
            grad_up_bias.reshape(rows_bias, count, cols_bias).transpose(1, 0, 2).reshape(count, -1),
            grad_qv.reshape(heads, count, cols_qv).transpose(1, 0, 2).reshape(count, -1),
        ],
        axis=1,
    )
    tail_rows = -(-small_grads.shape[1] // (16 * 3 * local)) * 16
    small_grads = jnp.pad(
        small_grads, ((0, 0), (0, tail_rows * 3 * local - small_grads.shape[1]))
    ).reshape(count, tail_rows, 3 * local)
    grad_qkv = matmul(ordered.reshape(-1, width), both(back_qkv_low), TN)
    tail = jnp.concatenate([grad_qkv.reshape(count, part, 3 * local), small_grads], axis=1)
    order = owners(index, count)
    tail = scatter_shards(
        [
            [lax.dynamic_index_in_dim(tail, order[step][flip], 0, keepdims=False) for flip in range(2)]
            for step in range(planes)
        ],
        count,
    )
    tail = tail.astype(BF16).astype(F32)
    small = tail[part:].reshape(-1)
    wide = small[: 6 * part].reshape(6, part)
    at = 6 * part
    up_bias_out = small[at : at + rows_bias * cols_bias].reshape(rows_bias, cols_bias)
    at = at + rows_bias * cols_bias
    qv_out = small[at : at + heads * cols_qv].reshape(heads, cols_qv)
    return (
        result,
        grad_tokens,
        tail[:part].reshape(part, 3, local),
        qv_out,
        bulk[part + lines :]
        .reshape(out_lines, local // out_lines, part)
        .transpose(1, 0, 2)
        .reshape(local, part),
        wide[0],
        wide[1],
        wide[2],
        bulk[:part],
        up_bias_out,
        bulk[part : part + lines]
        .reshape(lines, units // lines, part)
        .transpose(1, 0, 2)
        .reshape(units, part),
        wide[3],
        wide[4],
        wide[5],
    )


def solution(mesh):
    in_specs = (
        P("dp", None, None),
        P("dp", None, None),
        P("dp"),
        P("dp", None, "tensor"),
        P("tensor", "dp"),
        P("tensor", "dp"),
        P("dp"),
        P("dp"),
        P("dp"),
        P("dp", "tensor"),
        P("tensor", "dp"),
        P("tensor", "dp"),
        P("dp"),
        P("dp"),
        P("dp"),
    )
    out_specs = (
        P("dp", "tensor", None),
        P("dp", "tensor", None),
        P("dp", None, "tensor"),
        P("tensor", "dp"),
        P("tensor", "dp"),
        P("dp"),
        P("dp"),
        P("dp"),
        P("dp", "tensor"),
        P("tensor", "dp"),
        P("tensor", "dp"),
        P("dp"),
        P("dp"),
        P("dp"),
    )
    return jax.shard_map(body, mesh=mesh, in_specs=in_specs, out_specs=out_specs, check_vma=False)
```

```python
import math
from functools import partial

import jax
import jax.numpy as jnp
from jax import lax
from jax.experimental import pallas as pl
from jax.experimental.pallas import tpu as pltpu
from jax.sharding import PartitionSpec as P

EPSILON = 1e-12
NEG_LARGE = -1e30
F32 = jnp.float32
BF16 = jnp.bfloat16
LANES = 128
SMALL = 16
CHUNK = 256

ORDER = (0, 2, 1, 3)
CORE = [(i, i ^ 1) for i in range(4)]
SIDE = [(i, i ^ 2) for i in range(4)]
NN = ((1,), (0,))
NT = ((1,), (1,))
TN = ((0,), (0,))


def matmul(a, b, dims=NN):
    return lax.dot_general(a, b, (dims, ((), ())), preferred_element_type=F32)


def shaped(shape, dtype):
    return jax.ShapeDtypeStruct(shape, dtype)


def call(kernel, name, outs, tables, arrays, scratch=(), flops=0, spare=4):
    vmem = pl.BlockSpec(memory_space=pltpu.VMEM)
    smem = pl.BlockSpec(memory_space=pltpu.SMEM)
    moved = sum(a.size * a.dtype.itemsize for a in list(arrays) + list(outs))
    held = sum(math.prod(s.shape) * jnp.dtype(s.dtype).itemsize for s in scratch)
    with jax.named_scope(name):
        return pl.pallas_call(
            kernel,
            out_shape=tuple(outs),
            in_specs=[smem] * len(tables) + [vmem] * len(arrays),
            out_specs=tuple(vmem for _ in outs),
            scratch_shapes=list(scratch),
            cost_estimate=pl.CostEstimate(flops=flops, bytes_accessed=moved, transcendentals=0),
            compiler_params=pltpu.CompilerParams(vmem_limit_bytes=moved + held + spare * 2**20),
            name=name,
        )(*tables, *arrays)


def stack_rows(target, blocks):
    at = 0
    for block in blocks:
        target[at : at + block.shape[0], :] = block[...]
        at += block.shape[0]


def stack_cols(target, blocks):
    at = 0
    for block in blocks:
        target[:, at : at + block.shape[1]] = block[...]
        at += block.shape[1]


def pack_kernel(*refs, wide):
    qkv, up_bias, qv_bias = refs[0], refs[1 + wide], refs[2 + wide]
    out, small = refs[3 + wide :]
    part, local = qkv.shape[1:]
    for kind in range(qkv.shape[0]):
        out[:part, kind * local : (kind + 1) * local] = qkv[kind]
    small[...] = jnp.zeros(small.shape, F32)
    for row in range(wide):
        small[row : row + 1, :part] = refs[1 + row][...].astype(F32)
    for at, bias in ((LANES, up_bias), (2 * LANES, qv_bias)):
        small[: bias.shape[0], at : at + bias.shape[1]] = bias[...].astype(F32)
    out[part:, :] = jnp.zeros((SMALL, out.shape[1]), BF16)
    out[part:, : 3 * LANES] = small[...].astype(BF16)


def pack_first(qkv, wide, up_bias, qv_bias):
    kinds, part, local = qkv.shape
    return call(
        partial(pack_kernel, wide=len(wide)),
        "pack",
        [shaped((part + SMALL, kinds * local), BF16)],
        [],
        [qkv, *[w.reshape(1, -1) for w in wide], up_bias, qv_bias],
        [pltpu.VMEM((SMALL, 3 * LANES), F32)],
    )[0]


def reorder_kernel(spot, tokens, cotangent, *outs, share, part):
    seqs, length, width = tokens.shape
    for seq in range(seqs):
        ordered, own, upstream = outs[seq::seqs]
        for col in range(width // part):
            to = slice(col * part, (col + 1) * part)
            at = pl.ds(pl.multiple_of(spot[1 + col] * part, part), part)
            for block, step in enumerate(ORDER):
                rows = pl.ds(pl.multiple_of((spot[0] ^ step) * share, share), share)
                ordered[block * share : (block + 1) * share, to] = tokens[seq, rows, at]
                if block == 0:
                    own[:, to] = tokens[seq, rows, at]
                    upstream[:, to] = cotangent[seq, rows, at]


def reorder(spot, tokens, cotangent, share, part):
    seqs, length, width = tokens.shape
    if part % LANES:
        quarter = (seqs, len(ORDER), share, width // part, part)
        ordered = jnp.take(tokens.reshape(quarter), spot[0] ^ jnp.asarray(ORDER), axis=1)
        ordered = jnp.take(ordered, spot[1:], axis=3).reshape(tokens.shape)
        own = lax.dynamic_index_in_dim(cotangent.reshape(quarter), spot[0], 1, keepdims=False)
        own = jnp.take(own, spot[1:], axis=2).reshape(seqs, share, width)
        every = range(seqs)
        return (
            [ordered[s] for s in every],
            [ordered[s, :share] for s in every],
            [own[s] for s in every],
        )
    outs = call(
        partial(reorder_kernel, share=share, part=part),
        "reorder",
        [shaped((length, width), BF16)] * seqs + [shaped((share, width), BF16)] * (2 * seqs),
        [spot],
        [tokens, cotangent],
    )
    return outs[:seqs], outs[seqs : 2 * seqs], outs[2 * seqs :]


def put_columns(spot, out, value, part):
    for col in range(value.shape[-1] // part):
        at = pl.ds(pl.multiple_of(spot[1 + col] * part, part), part)
        out[:, at] = value[:, col * part : (col + 1) * part]


def restored(spot, array, part):
    if part % LANES == 0:
        return array
    split = array.reshape(array.shape[:-1] + (-1, part))
    return jnp.take(split, jnp.argsort(spot[1:]), axis=-2).reshape(array.shape)


def project_kernel(*refs, count, seqs, heads):
    spot, pieces, rows = refs[0], refs[1 : 1 + count], refs[1 + count : 1 + count + seqs]
    outs = refs[1 + count + seqs :]
    projs, (full, wide, up_row, bias, placed) = outs[:seqs], outs[seqs:]
    part = pieces[0].shape[0] - SMALL
    local = full.shape[1] // 3
    size = local // heads
    up = jnp.zeros((8, LANES), F32)
    qv = jnp.zeros((8, LANES), F32)
    for p, piece in enumerate(pieces):
        full[p * part : (p + 1) * part, :] = piece[:part, :]
        small = piece[part:, : 3 * LANES].astype(F32)
        wide[:, p * part : (p + 1) * part] = small[:8, :part]
        turn = spot[1 + p] * (LANES // count)
        up = up + pltpu.roll(small[:8, LANES : 2 * LANES], turn, axis=1)
        qv = qv + pltpu.roll(small[:8, 2 * LANES :], turn, axis=1)
    placed[...] = up
    for row in range(8):
        up_row[:, row * LANES : (row + 1) * LANES] = placed[row : row + 1, :]
    placed[...] = qv
    bias[...] = jnp.zeros(bias.shape, F32)
    lane = lax.broadcasted_iota(jnp.int32, (1, LANES), 1)
    for pair in range(heads // 2):
        low, high = placed[2 * pair : 2 * pair + 1, :], placed[2 * pair + 1 : 2 * pair + 2, :]
        at = slice(pair * LANES, (pair + 1) * LANES)
        bias[:, at] = jnp.where(lane < size, low, pltpu.roll(high, size, axis=1))
        at = slice(2 * local + pair * LANES, 2 * local + (pair + 1) * LANES)
        bias[:, at] = jnp.where(lane < size, pltpu.roll(low, size, axis=1), high)
    for seq in range(seqs):
        for at in range(0, 3 * local, CHUNK):
            cols = slice(at, at + CHUNK)
            projs[seq][:, cols] = (
                matmul(rows[seq][...], full[:, cols]) + bias[:, cols]
            ).astype(BF16)


def project(spot, pieces, rows, heads):
    seqs, count = len(rows), len(pieces)
    length, width = rows[0].shape
    wide = pieces[0].shape[1]
    outs = call(
        partial(project_kernel, count=count, seqs=seqs, heads=heads),
        "project",
        [shaped((length, wide), BF16)] * seqs
        + [shaped((width, wide), BF16), shaped((8, width), F32), shaped((1, 8 * LANES), F32)],
        [spot],
        [*pieces, *rows],
        [pltpu.VMEM((1, wide), F32), pltpu.VMEM((8, LANES), F32)],
        2 * seqs * length * width * wide,
    )
    return outs[:seqs], outs[seqs], outs[seqs + 1], outs[seqs + 2]


def positions(group, shape, axis, share):
    index = lax.broadcasted_iota(jnp.int32, shape, axis)
    block = index // share
    step = jnp.where(block == 1, 2, jnp.where(block == 2, 1, block))
    return (group ^ step) * share + index % share


def halves(product, cols, send, keep):
    rows = keep.shape[0]
    keep[:, cols] = product[:rows]
    send[:, cols] = product[rows:].astype(BF16)


def attend_kernel(*refs, heads, share, count):
    info, proj, pieces = refs[0], refs[1], refs[2 : 2 + count]
    context, send, keep, weight = refs[2 + count :]
    length, width = context.shape
    size = width // heads
    half = width // 2
    lane = lax.broadcasted_iota(jnp.int32, (1, width), 1)
    half_lane = lax.broadcasted_iota(jnp.int32, (1, half), 1)
    bias = jnp.where(positions(info[0], (1, length), 1, share) < info[1], 0.0, NEG_LARGE)
    scale = size ** (-0.5)
    queries = proj[:, :width]
    keys = proj[:, width : 2 * width]
    values = proj[:, 2 * width :]
    joined_halves = []
    for side in range(2):
        own = slice(side * half, (side + 1) * half)
        other = slice((1 - side) * half, (2 - side) * half)
        joined = jnp.zeros((length, half), F32)
        for inner in range(heads // 2):
            head = side * (heads // 2) + inner
            mine = (lane // size) == head
            scores = matmul(jnp.where(mine, queries, BF16(0)), keys, NT) * scale + bias
            terms = jnp.exp(scores).astype(BF16)
            summed = matmul(terms, jnp.where(mine, values, BF16(1)))
            joined = jnp.where(
                (half_lane // size) == inner, summed[:, own] / summed[:, other], joined
            )
        joined_halves.append(joined)
    context[...] = jnp.concatenate(joined_halves, axis=1).astype(BF16)
    stack_cols(weight, pieces)
    for at in range(0, weight.shape[1], CHUNK):
        cols = slice(at, at + CHUNK)
        halves(matmul(context[...], weight[:, cols]), cols, send, keep)


def attend(info, proj, pieces, heads, share):
    length, wide = proj.shape
    local = wide // 3
    width = sum(piece.shape[1] for piece in pieces)
    return call(
        partial(attend_kernel, heads=heads, share=share, count=len(pieces)),
        "attend",
        [
            shaped((length, local), BF16),
            shaped((length // 2, width), BF16),
            shaped((length // 2, width), F32),
        ],
        [info],
        [proj, *pieces],
        [pltpu.VMEM((local, width), BF16)],
        4 * length * length * local * heads + 2 * length * local * width,
        12,
    )


def attend_back_kernel(*refs, heads, share, count, blocks):
    info, proj, full = refs[0], refs[1], refs[2]
    pieces, back = refs[3 : 3 + count], refs[3 + count : 3 + count + blocks]
    grads, sums, send, keep, weight, rows = refs[3 + count + blocks :]
    length, wide = proj.shape
    width = wide // 3
    size = width // heads
    scale = size ** (-0.5)
    stack_cols(weight, pieces)
    stack_rows(rows, back)
    upstream = matmul(rows[...], weight[...], NT).astype(BF16)
    lane = lax.broadcasted_iota(jnp.int32, (1, width), 1)
    bias = jnp.where(positions(info[0], (length, 1), 0, share) < info[1], 0.0, NEG_LARGE)
    queries = proj[:, :width]
    keys = proj[:, width : 2 * width]
    values = proj[:, 2 * width :]
    zero = BF16(0)
    totals = [jnp.zeros((length, width), F32) for _ in range(3)]
    for head in range(heads):
        mine = (lane // size) == head
        head_q = jnp.where(mine, queries, zero)
        head_k = jnp.where(mine, keys, zero)
        head_up = jnp.where(mine, upstream, zero)
        terms = jnp.exp(matmul(keys, head_q, NT) * scale + bias)
        weights = terms * (1.0 / jnp.sum(terms, axis=0, keepdims=True))
        back_weights = matmul(values, head_up, NT)
        product = weights * back_weights
        scores = product - weights * jnp.sum(product, axis=0, keepdims=True)
        scores = (scores * scale).astype(BF16)
        totals[0] = totals[0] + matmul(scores, head_k, TN)
        totals[1] = totals[1] + matmul(scores, head_q)
        totals[2] = totals[2] + matmul(weights.astype(BF16), head_up)
    for kind in range(3):
        cols = slice(kind * width, (kind + 1) * width)
        sums[:, cols] = jnp.sum(totals[kind], axis=0, keepdims=True)
        grads[:, cols] = totals[kind].astype(BF16)
    for at in range(0, full.shape[0], CHUNK):
        cols = slice(at, at + CHUNK)
        halves(matmul(grads[...], full[cols, :], NT), cols, send, keep)


def attend_back(info, proj, full, pieces, back, heads, share):
    length, wide = proj.shape
    local = wide // 3
    width = full.shape[0]
    return call(
        partial(
            attend_back_kernel, heads=heads, share=share, count=len(pieces), blocks=len(back)
        ),
        "attend_back",
        [
            shaped((length, wide), BF16),
            shaped((1, wide), F32),
            shaped((length // 2, width), BF16),
            shaped((length // 2, width), F32),
        ],
        [info],
        [proj, full, *pieces, *back],
        [pltpu.VMEM((local, width), BF16), pltpu.VMEM((length, width), BF16)],
        10 * length * length * local * heads + 8 * length * local * width,
        16,
    )


def feed_kernel(*refs, count, blocks):
    parts, ups = refs[:blocks], refs[blocks : blocks + count]
    downs, bias = refs[blocks + count : blocks + 2 * count], refs[blocks + 2 * count]
    act, slope, send, keep, rows, up, down = refs[blocks + 2 * count + 1 :]
    stack_rows(rows, parts)
    stack_rows(up, ups)
    stack_cols(down, downs)
    for at in range(0, up.shape[1], CHUNK):
        cols = slice(at, at + CHUNK)
        pre = matmul(rows[...], up[:, cols]) + bias[:, cols]
        lower = 0.5 * (1.0 + lax.erf(pre * 0.7071067811865476))
        density = jnp.exp(-0.5 * pre * pre) * 0.3989422804014327
        act[:, cols] = (pre * lower).astype(BF16)
        slope[:, cols] = (lower + pre * density).astype(BF16)
    for at in range(0, down.shape[1], CHUNK):
        cols = slice(at, at + CHUNK)
        halves(matmul(act[...], down[:, cols]), cols, send, keep)


def feed_back_kernel(*refs, count, blocks):
    parts, ups = refs[:blocks], refs[blocks : blocks + count]
    downs, slope = refs[blocks + count : blocks + 2 * count], refs[blocks + 2 * count]
    back, sums, send, keep, rows, up, down = refs[blocks + 2 * count + 1 :]
    stack_rows(rows, parts)
    stack_rows(up, ups)
    stack_cols(down, downs)
    for at in range(0, up.shape[1], CHUNK):
        cols = slice(at, at + CHUNK)
        pre = matmul(rows[...], down[cols, :], NT) * slope[:, cols].astype(F32)
        sums[:, cols] = jnp.sum(pre, axis=0, keepdims=True)
        back[:, cols] = pre.astype(BF16)
    for at in range(0, down.shape[1], CHUNK):
        cols = slice(at, at + CHUNK)
        halves(matmul(back[...], up[cols, :], NT), cols, send, keep)


def feed(kernel, name, parts, ups, downs, extra, second):
    length = sum(part.shape[0] for part in parts)
    width, units = parts[0].shape[1], ups[0].shape[1]
    return call(
        partial(kernel, count=len(ups), blocks=len(parts)),
        name,
        [
            shaped((length, units), BF16),
            second,
            shaped((length // 2, width), BF16),
            shaped((length // 2, width), F32),
        ],
        [],
        [*parts, *ups, *downs, extra],
        [
            pltpu.VMEM((length, width), BF16),
            pltpu.VMEM((width, units), BF16),
            pltpu.VMEM((units, width), BF16),
        ],
        4 * length * width * units,
    )


OUT_BIAS, FIRST_GAIN, FIRST_SHIFT, DOWN_BIAS, SECOND_GAIN, SECOND_SHIFT = range(6)


def normalize(summed):
    centre = summed - jnp.mean(summed, axis=-1, keepdims=True)
    inverse = lax.rsqrt(jnp.mean(centre * centre, axis=-1, keepdims=True) + EPSILON)
    return centre * inverse, inverse


def norm_back(upstream, normed, inverse, gain):
    scaled = upstream * gain
    return inverse * (
        scaled
        - jnp.mean(scaled, axis=-1, keepdims=True)
        - normed * jnp.mean(scaled * normed, axis=-1, keepdims=True)
    )


def row_of(wide, row):
    return wide[row : row + 1, :]


def norm_one_kernel(keep, side, own, wide, low, normed_out, inverse_out):
    summed = own[...].astype(F32) + (keep[...] + side[...].astype(F32)) + row_of(wide, OUT_BIAS)
    normed, inverse = normalize(summed)
    hidden = normed * row_of(wide, FIRST_GAIN) + row_of(wide, FIRST_SHIFT)
    low[...] = hidden.astype(BF16)
    normed_out[...] = normed
    inverse_out[...] = inverse


def norm_two_kernel(
    info, spot, keep, side, normed_one, wide, cotangent, result, back_out, low, sums, *, part
):
    share = keep.shape[0]
    hidden = normed_one[...] * row_of(wide, FIRST_GAIN) + row_of(wide, FIRST_SHIFT)
    summed = hidden + (keep[...] + side[...].astype(F32)) + row_of(wide, DOWN_BIAS)
    normed, inverse = normalize(summed)
    gain = row_of(wide, SECOND_GAIN)
    valid = info[0] * share + lax.broadcasted_iota(jnp.int32, (share, 1), 0) < info[1]
    out = jnp.where(valid, normed * gain + row_of(wide, SECOND_SHIFT), 0.0).astype(BF16)
    if part % LANES:
        result[...] = out
    else:
        put_columns(spot, result, out, part)
    upstream = jnp.where(valid, cotangent[...].astype(F32), 0.0)
    back = norm_back(upstream, normed, inverse, gain)
    back_out[...] = back
    low[...] = back.astype(BF16)
    sums[0:1, :] = jnp.sum(back, axis=0, keepdims=True)
    sums[1:2, :] = jnp.sum(upstream * normed, axis=0, keepdims=True)
    sums[2:3, :] = jnp.sum(upstream, axis=0, keepdims=True)


def norm_back_kernel(keep, side, back_two, normed, inverse, wide, back_out, low, sums):
    upstream = back_two[...] + (keep[...] + side[...].astype(F32))
    back = norm_back(upstream, normed[...], inverse[...], row_of(wide, FIRST_GAIN))
    back_out[...] = back
    low[...] = back.astype(BF16)
    sums[0:1, :] = jnp.sum(back, axis=0, keepdims=True)
    sums[1:2, :] = jnp.sum(upstream * normed[...], axis=0, keepdims=True)
    sums[2:3, :] = jnp.sum(upstream, axis=0, keepdims=True)


def tokens_kernel(spot, *refs, seqs, part):
    out = refs[-1]
    for seq in range(seqs):
        back, keep, side = refs[3 * seq : 3 * seq + 3]
        total = back[...] + (keep[...] + side[...].astype(F32))
        if part % LANES:
            out[seq] = total
        else:
            put_columns(spot, out.at[seq], total, part)


def near_kernel(keep, there, own, send):
    share = own.shape[0]
    own[...] = keep[:share, :] + there[:share, :].astype(F32)
    send[...] = (keep[share:, :] + there[share:, :].astype(F32)).astype(BF16)


def scatter_rows(send, keep, tag):
    share, width = keep.shape[0] // 2, keep.shape[1]
    with jax.named_scope(f"{tag}_core"):
        there = lax.ppermute(send, "tensor", CORE)
    own, send = call(
        near_kernel,
        f"{tag}_near",
        [shaped((share, width), F32), shaped((share, width), BF16)],
        [],
        [keep, there],
    )
    with jax.named_scope(f"{tag}_side"):
        return own, lax.ppermute(send, "tensor", SIDE)


def gather_rows(own, tag):
    with jax.named_scope(f"{tag}_side"):
        side = lax.ppermute(own, "tensor", SIDE)
    with jax.named_scope(f"{tag}_core"):
        near = lax.ppermute(own, "tensor", CORE)
    with jax.named_scope(f"{tag}_far"):
        far = lax.ppermute(side, "tensor", CORE)
    return [own, side, near, far]


def tensor_sum(value):
    with jax.named_scope("sums_core"):
        value = value + lax.ppermute(value, "tensor", CORE)
    with jax.named_scope("sums_side"):
        return value + lax.ppermute(value, "tensor", SIDE)


def shard_order(index, count):
    planes = count // 2
    plane, side = index // 2, index % 2
    return [
        ((plane + planes - step) % planes) * 2 + (side ^ flip)
        for flip in range(2)
        for step in range(planes)
    ]


def pair_of(count):
    return [(i, i ^ 1) for i in range(count)]


def ring_of(step, count):
    return [(i, (i + 2 * step) % count) for i in range(count)]


def line_order(planes):
    return sorted(range(1, planes), key=lambda step: min(step, planes - step))


def gather_shards(shard, count, tag):
    planes = count // 2
    pieces = {0: shard}
    for step in line_order(planes):
        with jax.named_scope(f"{tag}_line{step}"):
            pieces[step] = lax.ppermute(shard, "dp", ring_of(step, count))
    far = []
    for step in range(planes):
        with jax.named_scope(f"{tag}_pair{step}"):
            far.append(lax.ppermute(pieces[step], "dp", pair_of(count)))
    return [pieces[step] for step in range(planes)] + far


def pair_sum_kernel(near, there, *outs):
    for step, out in enumerate(outs):
        out[...] = (near[step] + there[step].astype(F32)).astype(out.dtype)


def scatter_shards(near, far, count, tag):
    planes = count // 2
    with jax.named_scope(f"{tag}_pair"):
        there = lax.ppermute(far, "dp", pair_of(count))
    shape = near.shape[1:]
    summed = call(
        pair_sum_kernel,
        f"{tag}_sum",
        [shaped(shape, F32)] + [shaped(shape, BF16)] * (planes - 1),
        [],
        [near, there],
    )
    addends = [summed[0]]
    for step in line_order(planes):
        with jax.named_scope(f"{tag}_line{step}"):
            addends.append(lax.ppermute(summed[step], "dp", ring_of(planes - step, count)))
    return addends


def grad_kernel(*refs, left, right, by_rows):
    lefts, rights = refs[:left], refs[left : left + right]
    near, far, first, second = refs[left + right :]
    stack_rows(first, lefts)
    stack_rows(second, rights)
    planes, rows, cols = near.shape
    for at in range(0, second.shape[1], CHUNK):
        product = matmul(first[...], second[:, at : at + CHUNK], TN)
        if by_rows:
            for step in range(planes):
                for flip, out in enumerate((near, far)):
                    p = flip * planes + step
                    out[step, :, at : at + CHUNK] = product[p * rows : (p + 1) * rows].astype(
                        out.dtype
                    )
        else:
            for part in range(CHUNK // cols):
                p = at // cols + part
                out = (near, far)[p // planes]
                out[p % planes] = product[:, part * cols : (part + 1) * cols].astype(out.dtype)


def grad(name, lefts, rights, planes, by_rows):
    length = sum(a.shape[0] for a in lefts)
    rows, cols = lefts[0].shape[1], rights[0].shape[1]
    cut = (rows // (2 * planes), cols) if by_rows else (rows, cols // (2 * planes))
    return call(
        partial(grad_kernel, left=len(lefts), right=len(rights), by_rows=by_rows),
        name,
        [shaped((planes,) + cut, F32), shaped((planes,) + cut, BF16)],
        [],
        [*lefts, *rights],
        [pltpu.VMEM((length, rows), BF16), pltpu.VMEM((length, cols), BF16)],
        2 * length * rows * cols,
    )


def tail_kernel(*refs, seqs, blocks, count, heads):
    spot, refs = refs[0], refs[1:]
    rows, refs = refs[:seqs], refs[seqs:]
    backs, refs = refs[:seqs], refs[seqs:]
    ones, refs = refs[: seqs * blocks], refs[seqs * blocks :]
    contexts, refs = refs[:seqs], refs[seqs:]
    wide, refs = refs[0], refs[1:]
    unit_sums, refs = refs[:seqs], refs[seqs:]
    qkv_sums, refs = refs[:seqs], refs[seqs:]
    near, far, first, second, small, units, qv = refs
    planes = near.shape[0]
    part = near.shape[1] - SMALL
    local = contexts[0].shape[1]
    size = local // heads

    def store(at, product):
        for step in range(planes):
            for flip, out in enumerate((near, far)):
                p = flip * planes + step
                out[step, :part, at : at + product.shape[1]] = product[
                    p * part : (p + 1) * part
                ].astype(out.dtype)

    stack_rows(first, rows)
    for kind in range(3):
        cols = slice(kind * local, (kind + 1) * local)
        at = 0
        for back in backs:
            second[at : at + back.shape[0], :] = back[:, cols]
            at += back.shape[0]
        store(kind * local, matmul(first[...], second[...], TN))
    stack_rows(first, ones)
    stack_rows(second, contexts)
    store(3 * local, matmul(first[...], second[...], TN))

    unit_sum = unit_sums[0][...]
    qkv_sum = qkv_sums[0][...]
    for seq in range(1, seqs):
        unit_sum = unit_sum + unit_sums[seq][...]
        qkv_sum = qkv_sum + qkv_sums[seq][...]
    lane = lax.broadcasted_iota(jnp.int32, (1, LANES), 1)
    for row in range(8):
        units[row : row + 1, :] = unit_sum[:, row * LANES : (row + 1) * LANES]
    qv[...] = jnp.zeros(qv.shape, F32)
    for pair in range(heads // 2):
        at = pair * LANES
        queries = qkv_sum[:, at : at + LANES]
        values = qkv_sum[:, 2 * local + at : 2 * local + at + LANES]
        turned = pltpu.roll(queries, size, axis=1), pltpu.roll(values, size, axis=1)
        qv[2 * pair : 2 * pair + 1, :] = jnp.where(lane < size, queries, turned[1])
        qv[2 * pair + 1 : 2 * pair + 2, :] = jnp.where(lane < size, turned[0], values)
    for p in range(2 * planes):
        out = (near, far)[p // planes]
        turn = lax.rem(LANES - spot[1 + p] * (LANES // count), LANES)
        small[...] = jnp.zeros(small.shape, F32)
        small[:6, :part] = wide[:6, p * part : (p + 1) * part]
        small[:8, LANES : 2 * LANES] = pltpu.roll(units[...], turn, axis=1)
        small[:8, 2 * LANES :] = pltpu.roll(qv[...], turn, axis=1)
        out[p % planes, part:, :] = jnp.zeros((SMALL, out.shape[2]), out.dtype)
        out[p % planes, part:, : 3 * LANES] = small[...].astype(out.dtype)


def tail(spot, rows, backs, ones, contexts, wide, unit_sums, qkv_sums, count, heads):
    seqs, planes = len(rows), count // 2
    length, width = rows[0].shape
    local = contexts[0].shape[1]
    part = width // count
    shape = (planes, part + SMALL, 4 * local)
    return call(
        partial(tail_kernel, seqs=seqs, blocks=len(ones) // seqs, count=count, heads=heads),
        "tail",
        [shaped(shape, F32), shaped(shape, BF16)],
        [spot],
        [*rows, *backs, *ones, *contexts, wide, *unit_sums, *qkv_sums],
        [
            pltpu.VMEM((seqs * length, width), BF16),
            pltpu.VMEM((seqs * length, local), BF16),
            pltpu.VMEM((SMALL, 3 * LANES), F32),
            pltpu.VMEM((8, LANES), F32),
            pltpu.VMEM((8, LANES), F32),
        ],
        8 * seqs * length * width * local,
    )


def tail_out_kernel(*refs, addends):
    qkv, out, wide, units, qv = refs[addends:]
    kinds, part, local = qkv.shape
    total = refs[0][...]
    for addend in refs[1:addends]:
        total = total + addend[...].astype(F32)
    for kind in range(kinds):
        qkv[kind] = total[:part, kind * local : (kind + 1) * local]
    out[...] = total[:part, kinds * local :].T
    wide[...] = total[part : part + 8, :part]
    units[...] = total[part : part + units.shape[0], LANES : LANES + units.shape[1]]
    qv[...] = total[part : part + qv.shape[0], 2 * LANES : 2 * LANES + qv.shape[1]]


def added_kernel(*refs):
    total = refs[0][...]
    for addend in refs[1:-1]:
        total = total + addend[...].astype(F32)
    refs[-1][...] = total


def added(addends, name):
    return call(added_kernel, name, [shaped(addends[0].shape, F32)], [], addends)[0]


def sums_kernel(*refs, seqs):
    ones, twos, out = refs[:seqs], refs[seqs : 2 * seqs], refs[2 * seqs]
    out[...] = jnp.zeros(out.shape, F32)
    for at, group in ((0, ones), (3, twos)):
        total = group[0][...]
        for other in group[1:]:
            total = total + other[...]
        out[at : at + 3, :] = total[:3]


def body(
    tokens,
    cotangent,
    lengths,
    qkv_weight,
    qv_bias,
    out_weight,
    out_bias,
    first_gain,
    first_shift,
    up_weight,
    up_bias,
    down_weight,
    down_bias,
    second_gain,
    second_shift,
):
    seqs, length, width = tokens.shape
    groups = lax.axis_size("tensor")
    count = lax.axis_size("dp")
    planes = count // 2
    share = length // groups
    group = lax.axis_index("tensor")
    part = width // count
    local = qkv_weight.shape[2]
    units = up_weight.shape[1]
    heads = qv_bias.shape[0]
    every = range(seqs)
    order = jnp.stack(shard_order(lax.axis_index("dp"), count)).astype(jnp.int32)
    spot = jnp.concatenate([group.reshape(1).astype(jnp.int32), order])
    info = [jnp.stack([group, lengths[s]]).astype(jnp.int32) for s in every]

    wide_params = [out_bias, first_gain, first_shift, down_bias, second_gain, second_shift]
    first_pack = pack_first(qkv_weight.transpose(1, 0, 2), wide_params, up_bias, qv_bias)
    first = gather_shards(first_pack, count, "first")
    outs = gather_shards(out_weight, count, "outs")
    ups = gather_shards(up_weight, count, "ups")
    downs = gather_shards(down_weight, count, "downs")
    if part % LANES:
        outs = [jnp.concatenate(outs, axis=1)]
        ups = [jnp.concatenate(ups, axis=0)]
        downs = [jnp.concatenate(downs, axis=1)]

    ordered, own_tokens, own_cotangent = reorder(spot, tokens, cotangent, share, part)
    proj, qkv_full, wide, up_row = project(spot, first, ordered, heads)

    own = shaped((share, width), F32)
    own_low = shaped((share, width), BF16)
    sums = shaped((8, width), F32)
    context, result, act, slope, back, low_one, low_two = ([] for _ in range(7))
    normed, inverse, hidden, sums_one, sums_two = ([] for _ in range(5))
    for s in every:
        joined, send, keep = attend(info[s], proj[s], outs, heads, share)
        context.append(joined)
        keep, side = scatter_rows(send, keep, f"a{s}")
        low, z, q = call(
            norm_one_kernel,
            f"norm_one{s}",
            [own_low, own, shaped((share, 1), F32)],
            [],
            [keep, side, own_tokens[s], wide],
        )
        normed.append(z)
        inverse.append(q)
        hidden.append(gather_rows(low, f"b{s}"))
    back_two = []
    for s in every:
        active, inclined, send, keep = feed(
            feed_kernel,
            f"feed{s}",
            hidden[s],
            ups,
            downs,
            up_row,
            shaped((length, units), BF16),
        )
        act.append(active)
        slope.append(inclined)
        keep, side = scatter_rows(send, keep, f"c{s}")
        out, b, low, total = call(
            partial(norm_two_kernel, part=part),
            f"norm_two{s}",
            [own_low, own, own_low, sums],
            [info[s], spot],
            [keep, side, normed[s], wide, own_cotangent[s]],
        )
        result.append(out)
        back_two.append(b)
        sums_two.append(total)
        low_two.append(gather_rows(low, f"d{s}"))
    back_one, back_pre, unit_sums = [], [], []
    for s in every:
        b, total, send, keep = feed(
            feed_back_kernel,
            f"feed_back{s}",
            low_two[s],
            ups,
            downs,
            slope[s],
            shaped((1, units), F32),
        )
        back_pre.append(b)
        unit_sums.append(total)
        keep, side = scatter_rows(send, keep, f"e{s}")
        b, low, total = call(
            norm_back_kernel,
            f"norm_back{s}",
            [own, own_low, sums],
            [],
            [keep, side, back_two[s], normed[s], inverse[s], wide],
        )
        back_one.append(b)
        sums_one.append(total)
        low_one.append(gather_rows(low, f"f{s}"))

    flat = lambda blocks: [block for some in blocks for block in some]
    grad_down = scatter_shards(
        *grad("grad_down", act, flat(low_two), planes, False), count, "gdown"
    )
    grad_up = scatter_shards(
        *grad("grad_up", flat(hidden), back_pre, planes, True), count, "gup"
    )
    summed = call(
        partial(sums_kernel, seqs=seqs), "sums", [sums], [], [*sums_one, *sums_two]
    )[0]
    summed = tensor_sum(summed)

    back_qkv, qkv_sums, last = [], [], []
    for s in every:
        b, total, send, keep = attend_back(
            info[s], proj[s], qkv_full, outs, low_one[s], heads, share
        )
        back_qkv.append(b)
        qkv_sums.append(total)
        last += [back_one[s], *scatter_rows(send, keep, f"g{s}")]
    addends = scatter_shards(
        *tail(
            spot,
            ordered,
            back_qkv,
            flat(low_one),
            context,
            summed,
            unit_sums,
            qkv_sums,
            count,
            heads,
        ),
        count,
        "gtail",
    )
    grad_tokens = call(
        partial(tokens_kernel, seqs=seqs, part=part),
        "tokens",
        [shaped((seqs, share, width), F32)],
        [spot],
        last,
    )[0]
    grad_qkv, grad_out, small, grad_up_bias, grad_qv = call(
        partial(tail_out_kernel, addends=len(addends)),
        "tail_out",
        [
            shaped((3, part, local), F32),
            shaped(out_weight.shape, F32),
            shaped((8, part), F32),
            shaped(up_bias.shape, F32),
            shaped(qv_bias.shape, F32),
        ],
        [],
        addends,
    )
    return (
        restored(spot, jnp.stack(result), part),
        restored(spot, grad_tokens, part),
        grad_qkv.transpose(1, 0, 2),
        grad_qv,
        grad_out,
        small[OUT_BIAS],
        small[FIRST_GAIN],
        small[FIRST_SHIFT],
        added(grad_up, "up_out"),
        grad_up_bias,
        added(grad_down, "down_out"),
        small[DOWN_BIAS],
        small[SECOND_GAIN],
        small[SECOND_SHIFT],
    )


def solution(mesh):
    in_specs = (
        P("dp", None, None),
        P("dp", None, None),
        P("dp"),
        P("dp", None, "tensor"),
        P("tensor", "dp"),
        P("tensor", "dp"),
        P("dp"),
        P("dp"),
        P("dp"),
        P("dp", "tensor"),
        P("tensor", "dp"),
        P("tensor", "dp"),
        P("dp"),
        P("dp"),
        P("dp"),
    )
    out_specs = (
        P("dp", "tensor", None),
        P("dp", "tensor", None),
        P("dp", None, "tensor"),
        P("tensor", "dp"),
        P("tensor", "dp"),
        P("dp"),
        P("dp"),
        P("dp"),
        P("dp", "tensor"),
        P("tensor", "dp"),
        P("tensor", "dp"),
        P("dp"),
        P("dp"),
        P("dp"),
    )
    return jax.shard_map(body, mesh=mesh, in_specs=in_specs, out_specs=out_specs, check_vma=False)
```
